32 devices in a mesh: gx: 16 (over z, y, core), gy: 2 (over x).
Axes of the slice: x: 2, y: 2, z: 4, core: 2. Of those that a mesh axis runs over, the one named last changes fastest.
Arguments:
- state_field: bfloat16 [1, 64, 2048, 2048], P(None, None, 'gx', 'gy'), may hold values from -6 to 6
- spectral_x: bfloat16 [2, 32, 2, 64, 64], P(None, 'gx'), may hold values from -2 to 2
- spectral_y: bfloat16 [2, 32, 2, 64, 64], P(None, 'gy'), may hold values from -2 to 2
- expand_weight: bfloat16 [2, 64, 256], replicated, may hold values from -0.75 to 0.75
- reduce_weight: bfloat16 [2, 256, 64], replicated, may hold values from -0.375 to 0.375
Outputs:
- next_state: bfloat16 [1, 64, 2048, 2048], P(None, None, 'gx', 'gy')
The draws below stay inside these ranges and needn't reach their ends.
All inputs are finite; a program needn't handle non-finite values.
Results may differ from the reference program's by a relative error of at most 0.025.
Values may be sent and summed in bfloat16 or wider, within the bound.
A program may use at most 128 MiB of HBM per device.

```python
import jax
import jax.numpy as jnp
from jax import lax

NX = 2048
NY = 2048
CH = 64
HID = 256
MODES = 32
LAYERS = 2
ZP = 1


def shard_levels(rng, shape, shards, low, top_value):
    factor_of = 1.0
    for axis_at, blocks in shards:
        draws = jax.random.uniform(jax.random.fold_in(jax.random.fold_in(rng, 6), axis_at), (blocks,), jnp.float32, low / len(shards), top_value / len(shards))
        factor_of = factor_of * jnp.repeat(jnp.exp(draws), shape[axis_at] // blocks).reshape((-1,) + (1,) * (len(shape) - 1 - axis_at))
    return factor_of


def scatter_about(key, extent, width, reach, pieces=(), kind=jnp.bfloat16):
    values = jax.random.normal(key, extent, jnp.float32) * width
    if len(pieces) > 0:
        values = shard_levels(key, extent, pieces, -0.22, 0.18) * values
    return jnp.clip(values, min=-reach, max=reach).astype(kind)


def setup_inputs(seed: int = 0) -> dict:
    key_list = jax.random.split(jax.random.key(seed), 6)
    state_field = scatter_about(key_list[0], (ZP, CH, NX, NY), 1.0, 6.0, ((2, 16), (3, 2)))
    spectral_x = scatter_about(key_list[1], (LAYERS, MODES, 2, CH, CH), 8 ** -0.5, 2.0, ((1, 16),))
    spectral_y = scatter_about(key_list[2], (LAYERS, MODES, 2, CH, CH), 8 ** -0.5, 2.0, ((1, 2),))
    expand_weight = scatter_about(key_list[3], (LAYERS, CH, HID), CH ** -0.5, 0.75)
    reduce_weight = scatter_about(key_list[4], (LAYERS, HID, CH), HID ** -0.5, 0.375)
    return dict(state_field=state_field, spectral_x=spectral_x, spectral_y=spectral_y, expand_weight=expand_weight, reduce_weight=reduce_weight)


def make_tables(length, modes):
    positions = jnp.arange(length, dtype=jnp.int32)
    orders = jnp.arange(modes, dtype=jnp.int32)
    phase = orders[:, None] * positions[None, :] % length
    angle = 2.0 * jnp.pi * phase.astype(jnp.float32) / length
    factor = 1.0 / jnp.sqrt(jnp.float32(length))
    weight_two = jnp.where(orders == 0, 1.0, 2.0).astype(jnp.float32)[:, None]
    forward = jnp.stack([jnp.cos(angle) * factor, -jnp.sin(angle) * factor], axis=1)
    forward = forward.reshape(2 * modes, length).astype(jnp.bfloat16)
    inverse = jnp.stack([weight_two * jnp.cos(angle) * factor, -weight_two * jnp.sin(angle) * factor], axis=1)
    inverse = inverse.reshape(2 * modes, length).T.astype(jnp.bfloat16)
    return (forward, inverse)

def mix_modes(spectrum, weights):
    modes = weights.shape[0]
    shaped = spectrum.reshape((modes, 2) + spectrum.shape[1:]).astype(jnp.float32)
    weights = weights.astype(jnp.float32)
    real_in, imag_in = (shaped[:, 0], shaped[:, 1])
    real_w, imag_w = (weights[:, 0], weights[:, 1])

    def contract_modes(left, right):
        return jnp.einsum('koi,kzin->kzon', left, right)
    real_out = contract_modes(real_w, real_in) - contract_modes(imag_w, imag_in)
    imag_out = contract_modes(real_w, imag_in) + contract_modes(imag_w, real_in)
    joined = jnp.stack([real_out, imag_out], axis=1).astype(jnp.bfloat16)
    return joined.reshape(spectrum.shape)

def reference(state_field, spectral_x, spectral_y, expand_weight, reduce_weight):
    forward_x, inverse_x = make_tables(NX, MODES)
    forward_y, inverse_y = make_tables(NY, MODES)
    state = state_field
    block_rows = 128
    for layer_index in range(LAYERS):
        state_wide = state.astype(jnp.float32)
        spec_x = jnp.einsum('kx,zcxy->kzcy', forward_x.astype(jnp.float32), state_wide).astype(jnp.bfloat16)
        mixed_x = mix_modes(spec_x, spectral_x[layer_index])
        branch_x = jnp.einsum('xk,kzcy->zcxy', inverse_x.astype(jnp.float32), mixed_x.astype(jnp.float32)).astype(jnp.bfloat16)
        spec_y = jnp.einsum('ky,zcxy->kzcx', forward_y.astype(jnp.float32), state_wide).astype(jnp.bfloat16)
        mixed_y = mix_modes(spec_y, spectral_y[layer_index])
        branch_y = jnp.einsum('yk,kzcx->zcxy', inverse_y.astype(jnp.float32), mixed_y.astype(jnp.float32)).astype(jnp.bfloat16)
        total = (branch_x.astype(jnp.float32) + branch_y.astype(jnp.float32)).astype(jnp.bfloat16)
        expand_now = expand_weight[layer_index].astype(jnp.float32)
        reduce_now = reduce_weight[layer_index].astype(jnp.float32)
        blocks_total = jnp.moveaxis(total.reshape(ZP, CH, NX // block_rows, block_rows, NY), 2, 0)
        blocks_state = jnp.moveaxis(state.reshape(ZP, CH, NX // block_rows, block_rows, NY), 2, 0)

        def pointwise(pair):
            total_block, state_block = pair
            hidden = jax.nn.gelu(jnp.einsum('ch,zcxy->zhxy', expand_now, total_block.astype(jnp.float32)), approximate=True)
            hidden = hidden.astype(jnp.bfloat16).astype(jnp.float32)
            update = jnp.einsum('hc,zhxy->zcxy', reduce_now, hidden)
            return (state_block.astype(jnp.float32) + update).astype(jnp.bfloat16)
        result_blocks = lax.map(pointwise, (blocks_total, blocks_state))
        state = jnp.moveaxis(result_blocks, 0, 2).reshape(ZP, CH, NX, NY)
    return state
```

```python
import functools

import jax
import jax.numpy as jnp
from jax import lax
from jax.experimental import pallas as pl
from jax.experimental.pallas import tpu as pltpu
from jax.sharding import PartitionSpec as P

CHUNKS = 4
LANES = 128
GELU_A = 0.7978845608028654
GELU_B = 0.044715


def local_tables(first, count, length, modes):
    positions = first + jnp.arange(count, dtype=jnp.int32)
    orders = jnp.arange(modes, dtype=jnp.int32)
    phase = orders[:, None] * positions[None, :] % length
    angle = 2.0 * jnp.pi * phase.astype(jnp.float32) / length
    factor = 1.0 / jnp.sqrt(jnp.float32(length))
    weight_two = jnp.where(orders == 0, 1.0, 2.0).astype(jnp.float32)[:, None]
    real, imag = jnp.cos(angle) * factor, -jnp.sin(angle) * factor
    forward = jnp.stack([real, imag], axis=1).reshape(2 * modes, count)
    inverse = jnp.stack([weight_two * real, weight_two * imag], axis=1)
    inverse = inverse.reshape(2 * modes, count)
    return forward.astype(jnp.bfloat16), inverse.astype(jnp.bfloat16)


def dot(left, right):
    return jnp.dot(left, right, preferred_element_type=jnp.float32)


def group_spectra(base, news, fx, fyt, s_ref, acc_ref):
    rows2 = fx.shape[0]
    count, rows = len(news), news[0].shape[0]
    wide = dot(fx, jnp.concatenate(news, axis=1))
    for i in range(count):
        s_ref[pl.ds((base + i) * rows2, rows2), :] = wide[:, i * LANES : (i + 1) * LANES]
    tall = dot(jnp.concatenate(news, axis=0), fyt)
    for i in range(count):
        acc_ref[base + i] = acc_ref[base + i] + tall[i * rows : (i + 1) * rows]


def write_spectra(specx_ref, specy_ref, s_ref, acc_ref):
    rows2, channels, _ = specx_ref.shape
    for k in range(rows2):
        specx_ref[k] = s_ref[pl.ds(k, channels, stride=rows2), :].astype(jnp.bfloat16)

    @pl.when(pl.program_id(0) == pl.num_programs(0) - 1)
    def _():
        specy_ref[...] = acc_ref[...].astype(jnp.bfloat16)


def clear_first(acc_ref):
    @pl.when(pl.program_id(0) == 0)
    def _():
        acc_ref[...] = jnp.zeros_like(acc_ref)


def first_kernel(state_ref, fx_ref, fyt_ref, specx_ref, specy_ref, s_ref, acc_ref):
    clear_first(acc_ref)
    fx, fyt = fx_ref[...], fyt_ref[...]

    @pl.loop(0, state_ref.shape[0] // 4)
    def _(g):
        base = g * 4
        group_spectra(base, [state_ref[base + i] for i in range(4)], fx, fyt, s_ref, acc_ref)

    write_spectra(specx_ref, specy_ref, s_ref, acc_ref)


def layer_kernel(last, state_ref, mixed_ref, a_ref, iy_ref, w1_ref, w2_ref, *refs):
    if last:
        out_ref, m_ref, t_ref = refs[-3:]
    else:
        fx_ref, fyt_ref, out_ref, specx_ref, specy_ref, m_ref, t_ref, s_ref, acc_ref = refs
        clear_first(acc_ref)
        fx, fyt = fx_ref[...], fyt_ref[...]
    channels, rows, _ = state_ref.shape
    rows2 = mixed_ref.shape[0]
    for k in range(rows2):
        m_ref[pl.ds(k * channels, channels), :] = mixed_ref[k].astype(jnp.float32)
    iy = iy_ref[...]

    @pl.loop(0, channels // 4)
    def _(g):
        for i in range(4):
            c = g * 4 + i
            part = m_ref[pl.ds(c, rows2, stride=channels), :].astype(jnp.bfloat16)
            t_ref[pl.ds(c * rows, rows), :] = dot(a_ref[c], jnp.concatenate([part, iy], axis=0))

    w1, w2 = w1_ref[...], w2_ref[...]
    ca = jnp.bfloat16(GELU_A)
    cb = jnp.bfloat16(GELU_A * GELU_B)

    @pl.loop(0, rows // 8)
    def _(g):
        for j in range(2):
            base = g * 8 + j * 4
            parts = [t_ref[pl.ds(base + i, channels, stride=rows), :] for i in range(4)]
            h = dot(w1, jnp.concatenate(parts, axis=1).astype(jnp.bfloat16)).astype(jnp.bfloat16)
            th = jnp.tanh(h * (ca + cb * (h * h)))
            u = dot(w2, h + h * th)
            for i in range(4):
                t_ref[pl.ds(base + i, channels, stride=rows), :] = u[:, i * LANES : (i + 1) * LANES]

    @pl.loop(0, channels // 4)
    def _(g):
        base = g * 4
        news = []
        for i in range(4):
            c = base + i
            new = state_ref[c].astype(jnp.float32) + t_ref[pl.ds(c * rows, rows), :]
            new = new.astype(jnp.bfloat16)
            out_ref[c] = new
            news.append(new)
        if not last:
            group_spectra(base, news, fx, fyt, s_ref, acc_ref)

    if not last:
        write_spectra(specx_ref, specy_ref, s_ref, acc_ref)


def whole(array):
    zeros = (0,) * array.ndim
    return pl.BlockSpec(array.shape, lambda j: zeros)


def body(state_field, spectral_x, spectral_y, expand_weight, reduce_weight):
    planes, channels, rows, cols = state_field.shape
    layers, hidden = expand_weight.shape[0], expand_weight.shape[2]
    nx, ny = rows * lax.axis_size("gx"), cols * lax.axis_size("gy")
    modes = spectral_x.shape[1] * lax.axis_size("gx")
    rows2 = 2 * modes
    chunks = CHUNKS if cols % (CHUNKS * LANES) == 0 else cols // LANES
    width = cols // chunks
    steps = width // LANES
    forward_x, inverse_x = local_tables(lax.axis_index("gx") * rows, rows, nx, modes)
    forward_y, inverse_y = local_tables(lax.axis_index("gy") * cols, cols, ny, modes)
    forward_yt = forward_y.T
    inverse_xt = inverse_x.T

    def block_matrix(w):
        top = jnp.concatenate([w[..., 0, :, :], -w[..., 1, :, :]], axis=-1)
        low = jnp.concatenate([w[..., 1, :, :], w[..., 0, :, :]], axis=-1)
        return jnp.concatenate([top, low], axis=-2)

    mat_x = block_matrix(spectral_x)
    mat_y = block_matrix(lax.all_gather(spectral_y, "gy", axis=1, tiled=True))

    bf16 = jnp.bfloat16
    s_scr = pltpu.VMEM((channels * rows2, LANES), jnp.float32)
    m_scr = pltpu.VMEM((rows2 * channels, LANES), jnp.float32)
    t_scr = pltpu.VMEM((channels * rows, LANES), jnp.float32)
    acc_scr = pltpu.VMEM((channels, rows, rows2), jnp.float32)
    specx_shape = jax.ShapeDtypeStruct((rows2, channels, width), bf16)
    specx_spec = pl.BlockSpec((rows2, channels, LANES), lambda j: (0, 0, j))
    specy_shape = jax.ShapeDtypeStruct((channels, rows, rows2), bf16)
    specy_spec = pl.BlockSpec((channels, rows, rows2), lambda j: (0, 0, 0))
    params = pltpu.CompilerParams(
        dimension_semantics=("arbitrary",), vmem_limit_bytes=56 * 1024 * 1024
    )
    cells = rows * width

    def cost(flops, moved):
        return pl.CostEstimate(flops=flops, bytes_accessed=moved, transcendentals=0)

    def at(first):
        return pl.BlockSpec((channels, rows, LANES), lambda j: (0, 0, j + first))

    def fyt_spec(first):
        return pl.BlockSpec((LANES, rows2), lambda j: (j + first, 0))

    spectra_flops = 4 * rows2 * channels * cells

    def first_call(state, n):
        return pl.pallas_call(
            first_kernel,
            name="spectra",
            grid=(steps,),
            in_specs=[at(n * steps), whole(forward_x), fyt_spec(n * steps)],
            out_specs=[specx_spec, specy_spec],
            out_shape=[specx_shape, specy_shape],
            scratch_shapes=[s_scr, acc_scr],
            compiler_params=params,
            cost_estimate=cost(spectra_flops, 4 * channels * cells),
        )(state, forward_x, forward_yt)

    def layer_call(last, state, first, n, mixed, a, w1, w2, result):
        ins = [state, mixed, a, inverse_y, w1, w2]
        specs = [
            at(first),
            specx_spec,
            whole(a),
            pl.BlockSpec((rows2, LANES), lambda j: (0, j + n * steps)),
            whole(w1),
            whole(w2),
        ]
        aliases = {}
        scratch = [m_scr, t_scr]
        if last:
            out_shape = [jax.ShapeDtypeStruct((channels, rows, cols), bf16)]
            out_specs = [at(n * steps)]
            if result is not None:
                aliases = {len(ins): 0}
                ins.append(result)
                specs.append(pl.BlockSpec(memory_space=pl.ANY))
        else:
            ins += [forward_x, forward_yt]
            specs += [whole(forward_x), fyt_spec(n * steps)]
            out_shape = [jax.ShapeDtypeStruct((channels, rows, width), bf16), specx_shape, specy_shape]
            out_specs = [at(0), specx_spec, specy_spec]
            scratch += [s_scr, acc_scr]
        flops = (4 * channels * hidden * 2 + 8 * rows2 * channels) * cells
        return pl.pallas_call(
            functools.partial(layer_kernel, last),
            name="layer_last" if last else "layer",
            grid=(steps,),
            in_specs=specs,
            out_specs=out_specs,
            out_shape=out_shape,
            scratch_shapes=scratch,
            input_output_aliases=aliases,
            compiler_params=params,
            cost_estimate=cost(flops, 8 * channels * cells),
        )(*ins)

    state = state_field.reshape(channels, rows, cols)
    pieces = [(state, n * steps) for n in range(chunks)]
    spectra = [first_call(state, n) for n in range(chunks)]
    for layer in range(layers):
        last = layer == layers - 1
        owned = [lax.psum_scatter(s, "gx", scatter_dimension=0, tiled=True) for s, _ in spectra]
        mixed = []
        for part in owned:
            pairs = part.reshape(part.shape[0] // 2, 2 * channels, width)
            product = jnp.einsum(
                "moi,miy->moy", mat_x[layer], pairs, preferred_element_type=jnp.float32
            )
            product = product.astype(bf16).reshape(part.shape)
            mixed.append(lax.all_gather(product, "gx", axis=0, tiled=True))
        spec_y = sum(s.astype(jnp.float32) for _, s in spectra).astype(bf16)
        spec_y = lax.psum(jnp.transpose(spec_y, (2, 0, 1)), "gy")
        mixed_y = jnp.einsum(
            "moi,mix->mox",
            mat_y[layer],
            spec_y.reshape(modes, 2 * channels, rows),
            preferred_element_type=jnp.float32,
        ).astype(bf16)
        mixed_y = jnp.transpose(mixed_y.reshape(rows2, channels, rows), (1, 2, 0))
        a = jnp.concatenate(
            [jnp.broadcast_to(inverse_xt[None], (channels, rows, rows2)), mixed_y], axis=2
        )
        w1 = expand_weight[layer].T
        w2 = (reduce_weight[layer].astype(jnp.float32) * 0.5).astype(bf16).T
        result, next_pieces, next_spectra = None, [], []
        for n in range(chunks):
            source, first = pieces[n]
            outs = layer_call(last, source, first, n, mixed[n], a, w1, w2, result)
            if last:
                result = outs[0]
            else:
                next_pieces.append((outs[0], 0))
                next_spectra.append((outs[1], outs[2]))
        pieces, spectra = next_pieces, next_spectra
    return result.reshape(state_field.shape)


def solution(mesh):
    in_specs = (
        P(None, None, "gx", "gy"),
        P(None, "gx", None, None, None),
        P(None, "gy", None, None, None),
        P(),
        P(),
    )
    out_specs = P(None, None, "gx", "gy")
    return jax.shard_map(body, mesh=mesh, in_specs=in_specs, out_specs=out_specs, check_vma=False)
```

```python
import functools

import jax
import jax.numpy as jnp
from jax import lax
from jax.experimental import pallas as pl
from jax.experimental.pallas import tpu as pltpu
from jax.sharding import PartitionSpec as P

CHUNKS = 2
LANES = 128
GELU_A = 0.7978845608028654
GELU_B = 0.044715


def local_tables(first, count, length, modes):
    positions = first + jnp.arange(count, dtype=jnp.int32)
    orders = jnp.arange(modes, dtype=jnp.int32)
    phase = orders[:, None] * positions[None, :] % length
    angle = 2.0 * jnp.pi * phase.astype(jnp.float32) / length
    factor = 1.0 / jnp.sqrt(jnp.float32(length))
    weight_two = jnp.where(orders == 0, 1.0, 2.0).astype(jnp.float32)[:, None]
    real, imag = jnp.cos(angle) * factor, -jnp.sin(angle) * factor
    forward = jnp.stack([real, imag], axis=1).reshape(2 * modes, count)
    inverse = jnp.stack([weight_two * real, weight_two * imag], axis=1)
    inverse = inverse.reshape(2 * modes, count)
    return forward.astype(jnp.bfloat16), inverse.astype(jnp.bfloat16)


def dot(left, right):
    return jnp.dot(left, right, preferred_element_type=jnp.float32)


def group_spectra(base, news, fx, fyt, s_ref, acc_ref):
    rows2 = fx.shape[0]
    count, rows = len(news), news[0].shape[0]
    wide = dot(fx, jnp.concatenate(news, axis=1))
    for i in range(count):
        s_ref[pl.ds((base + i) * rows2, rows2), :] = wide[:, i * LANES : (i + 1) * LANES]
    tall = dot(jnp.concatenate(news, axis=0), fyt)
    for i in range(count):
        acc_ref[base + i] = acc_ref[base + i] + tall[i * rows : (i + 1) * rows]


def write_spectra(specx_ref, specy_ref, s_ref, acc_ref):
    rows2, channels, _ = specx_ref.shape
    for k in range(rows2):
        specx_ref[k] = s_ref[pl.ds(k, channels, stride=rows2), :].astype(jnp.bfloat16)

    @pl.when(pl.program_id(0) == pl.num_programs(0) - 1)
    def _():
        specy_ref[...] = acc_ref[...].astype(jnp.bfloat16)


def clear_first(acc_ref):
    @pl.when(pl.program_id(0) == 0)
    def _():
        acc_ref[...] = jnp.zeros_like(acc_ref)


def first_kernel(state_ref, fx_ref, fyt_ref, specx_ref, specy_ref, s_ref, acc_ref):
    clear_first(acc_ref)
    fx, fyt = fx_ref[...], fyt_ref[...]

    @pl.loop(0, state_ref.shape[0] // 4)
    def _(g):
        base = g * 4
        group_spectra(base, [state_ref[base + i] for i in range(4)], fx, fyt, s_ref, acc_ref)

    write_spectra(specx_ref, specy_ref, s_ref, acc_ref)


def layer_kernel(last, state_ref, mixed_ref, a_ref, iy_ref, w1_ref, w2_ref, *refs):
    if last:
        out_ref, m_ref, t_ref = refs[-3:]
    else:
        fx_ref, fyt_ref, out_ref, specx_ref, specy_ref, m_ref, t_ref, s_ref, acc_ref = refs
        clear_first(acc_ref)
        fx, fyt = fx_ref[...], fyt_ref[...]
    channels, rows, _ = state_ref.shape
    rows2 = mixed_ref.shape[0]
    for k in range(rows2):
        m_ref[pl.ds(k * channels, channels), :] = mixed_ref[k].astype(jnp.float32)
    iy = iy_ref[...]

    @pl.loop(0, channels // 4)
    def _(g):
        for i in range(4):
            c = g * 4 + i
            part = m_ref[pl.ds(c, rows2, stride=channels), :].astype(jnp.bfloat16)
            t_ref[pl.ds(c * rows, rows), :] = dot(a_ref[c], jnp.concatenate([part, iy], axis=0))

    w1, w2 = w1_ref[...], w2_ref[...]
    ca = jnp.bfloat16(GELU_A)
    cb = jnp.bfloat16(GELU_A * GELU_B)

    @pl.loop(0, rows // 8)
    def _(g):
        for j in range(2):
            base = g * 8 + j * 4
            parts = [t_ref[pl.ds(base + i, channels, stride=rows), :] for i in range(4)]
            h = dot(w1, jnp.concatenate(parts, axis=1).astype(jnp.bfloat16)).astype(jnp.bfloat16)
            th = jnp.tanh(h * (ca + cb * (h * h)))
            u = dot(w2, h + h * th)
            for i in range(4):
                t_ref[pl.ds(base + i, channels, stride=rows), :] = u[:, i * LANES : (i + 1) * LANES]

    @pl.loop(0, channels // 4)
    def _(g):
        base = g * 4
        news = []
        for i in range(4):
            c = base + i
            new = state_ref[c].astype(jnp.float32) + t_ref[pl.ds(c * rows, rows), :]
            new = new.astype(jnp.bfloat16)
            out_ref[c] = new
            news.append(new)
        if not last:
            group_spectra(base, news, fx, fyt, s_ref, acc_ref)

    if not last:
        write_spectra(specx_ref, specy_ref, s_ref, acc_ref)


def whole(array):
    zeros = (0,) * array.ndim
    return pl.BlockSpec(array.shape, lambda j: zeros)


def body(state_field, spectral_x, spectral_y, expand_weight, reduce_weight):
    planes, channels, rows, cols = state_field.shape
    layers, hidden = expand_weight.shape[0], expand_weight.shape[2]
    nx, ny = rows * lax.axis_size("gx"), cols * lax.axis_size("gy")
    modes = spectral_x.shape[1] * lax.axis_size("gx")
    rows2 = 2 * modes
    chunks = CHUNKS if cols % (CHUNKS * LANES) == 0 else cols // LANES
    width = cols // chunks
    steps = width // LANES
    forward_x, inverse_x = local_tables(lax.axis_index("gx") * rows, rows, nx, modes)
    forward_y, inverse_y = local_tables(lax.axis_index("gy") * cols, cols, ny, modes)
    forward_yt = forward_y.T
    inverse_xt = inverse_x.T

    def block_matrix(w):
        top = jnp.concatenate([w[..., 0, :, :], -w[..., 1, :, :]], axis=-1)
        low = jnp.concatenate([w[..., 1, :, :], w[..., 0, :, :]], axis=-1)
        return jnp.concatenate([top, low], axis=-2)

    mat_x = block_matrix(spectral_x)
    mat_y = block_matrix(lax.all_gather(spectral_y, "gy", axis=1, tiled=True))

    bf16 = jnp.bfloat16
    s_scr = pltpu.VMEM((channels * rows2, LANES), jnp.float32)
    m_scr = pltpu.VMEM((rows2 * channels, LANES), jnp.float32)
    t_scr = pltpu.VMEM((channels * rows, LANES), jnp.float32)
    acc_scr = pltpu.VMEM((channels, rows, rows2), jnp.float32)
    specx_shape = jax.ShapeDtypeStruct((rows2, channels, width), bf16)
    specx_spec = pl.BlockSpec((rows2, channels, LANES), lambda j: (0, 0, j))
    specy_shape = jax.ShapeDtypeStruct((channels, rows, rows2), bf16)
    specy_spec = pl.BlockSpec((channels, rows, rows2), lambda j: (0, 0, 0))
    params = pltpu.CompilerParams(
        dimension_semantics=("arbitrary",), vmem_limit_bytes=56 * 1024 * 1024
    )
    cells = rows * width

    def cost(flops, moved):
        return pl.CostEstimate(flops=flops, bytes_accessed=moved, transcendentals=0)

    def at(first):
        return pl.BlockSpec((channels, rows, LANES), lambda j: (0, 0, j + first))

    def fyt_spec(first):
        return pl.BlockSpec((LANES, rows2), lambda j: (j + first, 0))

    spectra_flops = 4 * rows2 * channels * cells

    def first_call(state, n):
        return pl.pallas_call(
            first_kernel,
            name="spectra",
            grid=(steps,),
            in_specs=[at(n * steps), whole(forward_x), fyt_spec(n * steps)],
            out_specs=[specx_spec, specy_spec],
            out_shape=[specx_shape, specy_shape],
            scratch_shapes=[s_scr, acc_scr],
            compiler_params=params,
            cost_estimate=cost(spectra_flops, 4 * channels * cells),
        )(state, forward_x, forward_yt)

    def layer_call(last, state, first, n, mixed, a, w1, w2, result):
        ins = [state, mixed, a, inverse_y, w1, w2]
        specs = [
            at(first),
            specx_spec,
            whole(a),
            pl.BlockSpec((rows2, LANES), lambda j: (0, j + n * steps)),
            whole(w1),
            whole(w2),
        ]
        aliases = {}
        scratch = [m_scr, t_scr]
        if last:
            out_shape = [jax.ShapeDtypeStruct((channels, rows, cols), bf16)]
            out_specs = [at(n * steps)]
            if result is not None:
                aliases = {len(ins): 0}
                ins.append(result)
                specs.append(pl.BlockSpec(memory_space=pl.ANY))
        else:
            ins += [forward_x, forward_yt]
            specs += [whole(forward_x), fyt_spec(n * steps)]
            out_shape = [jax.ShapeDtypeStruct((channels, rows, width), bf16), specx_shape, specy_shape]
            out_specs = [at(0), specx_spec, specy_spec]
            scratch += [s_scr, acc_scr]
        flops = (4 * channels * hidden * 2 + 8 * rows2 * channels) * cells
        return pl.pallas_call(
            functools.partial(layer_kernel, last),
            name="layer_last" if last else "layer",
            grid=(steps,),
            in_specs=specs,
            out_specs=out_specs,
            out_shape=out_shape,
            scratch_shapes=scratch,
            input_output_aliases=aliases,
            compiler_params=params,
            cost_estimate=cost(flops, 8 * channels * cells),
        )(*ins)

    state = state_field.reshape(channels, rows, cols)
    pieces = [(state, n * steps) for n in range(chunks)]
    spectra = [first_call(state, n) for n in range(chunks)]
    for layer in range(layers):
        last = layer == layers - 1
        owned = [lax.psum_scatter(s, "gx", scatter_dimension=0, tiled=True) for s, _ in spectra]
        mixed = []
        for part in owned:
            pairs = part.reshape(part.shape[0] // 2, 2 * channels, width)
            product = jnp.einsum(
                "moi,miy->moy", mat_x[layer], pairs, preferred_element_type=jnp.float32
            )
            product = product.astype(bf16).reshape(part.shape)
            mixed.append(lax.all_gather(product, "gx", axis=0, tiled=True))
        spec_y = sum(s.astype(jnp.float32) for _, s in spectra).astype(bf16)
        spec_y = lax.psum(jnp.transpose(spec_y, (2, 0, 1)), "gy")
        mixed_y = jnp.einsum(
            "moi,mix->mox",
            mat_y[layer],
            spec_y.reshape(modes, 2 * channels, rows),
            preferred_element_type=jnp.float32,
        ).astype(bf16)
        mixed_y = jnp.transpose(mixed_y.reshape(rows2, channels, rows), (1, 2, 0))
        a = jnp.concatenate(
            [jnp.broadcast_to(inverse_xt[None], (channels, rows, rows2)), mixed_y], axis=2
        )
        w1 = expand_weight[layer].T
        w2 = (reduce_weight[layer].astype(jnp.float32) * 0.5).astype(bf16).T
        result, next_pieces, next_spectra = None, [], []
        for n in range(chunks):
            source, first = pieces[n]
            outs = layer_call(last, source, first, n, mixed[n], a, w1, w2, result)
            if last:
                result = outs[0]
            else:
                next_pieces.append((outs[0], 0))
                next_spectra.append((outs[1], outs[2]))
        pieces, spectra = next_pieces, next_spectra
    return result.reshape(state_field.shape)


def solution(mesh):
    in_specs = (
        P(None, None, "gx", "gy"),
        P(None, "gx", None, None, None),
        P(None, "gy", None, None, None),
        P(),
        P(),
    )
    out_specs = P(None, None, "gx", "gy")
    return jax.shard_map(body, mesh=mesh, in_specs=in_specs, out_specs=out_specs, check_vma=False)
```
